32 devices in a mesh: prow: 4 (over y, core), pcol: 8 (over z, x).
Axes of the slice: x: 2, y: 2, z: 4, core: 2. Of those that a mesh axis runs over, the one named last changes fastest.
Arguments:
- ainv: bfloat16 [8192, 8192], P('prow', 'pcol'), may hold values from -6 to 6
- panels: bfloat16 [3, 8192, 128], P(None, ('prow', 'pcol')), may hold values from -0.0625 to 0.0625
- structure: int32 [3, 64], replicated, may hold values from 0 to 1, as said below
- dinv: float32 [3, 128, 128], replicated, may hold values from -6 to 6
- couple: bfloat16 [2, 128, 128], replicated, may hold values from -0.5 to 0.5
Outputs:
- inv_panels: float32 [3, 8192, 128], P(None, ('prow', 'pcol'))
- inv_parent: float32 [2, 128, 128], replicated
- inv_diag: float32 [3, 128, 128], replicated
The draws below stay inside these ranges and needn't reach their ends.
Inputs may be any that keep to these rules, and one draw needn't show every extreme that they name: Entries are 0 or 1; a block in the structure of step k+1 is also in that of step k.
All inputs are finite; a program needn't handle non-finite values.
Results may differ from the reference program's by a relative error of at most 0.0003.
Values may be sent and summed in bfloat16 or wider, within the bound.
No kernel may reach another device: no remote copies, remote signals or barrier semaphores. Data moves between devices by JAX's collectives and lax.ppermute only.
A program may use at most 64 MiB of HBM per device.

```python
import jax
import jax.numpy as jnp
from jax import lax

W = 128
BLK_COL = 8
STEPS = 3
NBLK = 64
NBW = 8192
N_PCOL = 8


def draw_structure(key, part):
    levels = jax.random.randint(key, (NBLK,), 0, STEPS + 1)
    levels = levels.at[0].set(STEPS).at[1].set(0)
    sections = jnp.arange(STEPS, dtype=jnp.int32)
    return (levels[None, :] > sections[:, None]).astype(jnp.int32)


def spiked(values, own_key, source, target, parts, factor):
    def block_of(dim):
        return (jnp.arange(values.shape[dim]) // (values.shape[dim] // parts)).reshape((-1,) + (1,) * (values.ndim - 1 - dim))

    first = jax.random.permutation(own_key, parts)[block_of(target)]
    far = (block_of(target) + parts // 2) % parts
    return jnp.where((block_of(source) == first) | (block_of(source) == far), factor * values, values)


def shard_levels(own_key, extent, shards, least, top_value):
    gain, own = 1.0, jax.random.fold_in(own_key, 6)
    for axis_at, blocks in shards:
        steps = jnp.exp(jax.random.uniform(jax.random.fold_in(own, axis_at), (blocks,), jnp.float32, least / len(shards), top_value / len(shards)))
        gain = gain * jnp.repeat(steps, extent[axis_at] // blocks).reshape([-1 if axis == axis_at else 1 for axis in range(len(extent))])
    return gain


def normal_values(stream_key, dims, width, reach, pieces=(), held_as=jnp.bfloat16):
    drawn = jax.random.normal(stream_key, dims, jnp.float32) * width
    if len(pieces) > 0:
        drawn = shard_levels(stream_key, dims, pieces, -0.22, 0.18) * drawn
    return jnp.clip(drawn, min=-reach, max=reach).astype(held_as)


def noise_with(rng, extent, spread, limit, pieces, heavy, held_as=jnp.bfloat16):
    array = spread * jax.random.normal(rng, extent, jnp.float32)
    if pieces:
        array = array * shard_levels(rng, extent, pieces, -0.22, 0.18)
    return jnp.clip(spiked(array, jax.random.fold_in(rng, 3), *heavy), -limit, limit).astype(held_as)


def setup_inputs(seed: int = 0) -> dict:
    keys = jax.random.split(jax.random.key(seed), 6)
    return {
        "ainv": noise_with(keys[0], (NBW, NBW), 1.0, 6.0, ((0, 4), (1, 8)), (1, 0, 8, 2.0)),
        "panels": normal_values(keys[1], (STEPS, NBW, W), (NBLK * W) ** -0.5, 0.0625, ((1, 32),)),
        "structure": draw_structure(jax.random.fold_in(keys[5], 71), 0),
        "dinv": normal_values(keys[3], (STEPS, W, W), 1.0, 6.0, (), jnp.float32),
        "couple": normal_values(keys[4], (STEPS - 1, W, W), W ** -0.5, 0.5),
    }


def reference(ainv, panels, structure, dinv, couple):
    high = lax.Precision.HIGHEST
    live_rows = jnp.repeat(structure.astype(jnp.float32), W, axis=1)
    factor = panels * live_rows[:, :, None].astype(jnp.bfloat16)
    factor_wide = factor.astype(jnp.float32)
    strips = ainv.reshape(N_PCOL, BLK_COL * W, NBLK * W)

    def strip_product(strip):
        return jnp.einsum("rc,kcw->krw", strip.astype(jnp.float32), factor_wide, precision=high)

    products = lax.map(strip_product, strips)
    products = jnp.transpose(products, (1, 0, 2, 3)).reshape(STEPS, NBLK * W, W)
    couple_wide = couple.astype(jnp.float32)
    first_block = -products[0] * live_rows[0][:, None]
    diag_now = dinv[0] - jnp.dot(factor_wide[0].T, first_block, precision=high)
    blocks_out = [first_block]
    diag_out = [diag_now]
    cross_out = []
    for section in range(1, STEPS):
        previous = blocks_out[-1]
        current = -(products[section] + jnp.dot(previous, couple_wide[section - 1], precision=high)) * live_rows[section][:, None]
        own_sum = jnp.dot(factor_wide[section].T, current, precision=high)
        cross_sum = jnp.dot(previous.T, factor_wide[section], precision=high)
        cross = -(cross_sum + jnp.dot(diag_now, couple_wide[section - 1], precision=high))
        diag_now = dinv[section] - own_sum - jnp.dot(couple_wide[section - 1].T, cross, precision=high)
        blocks_out.append(current)
        cross_out.append(cross)
        diag_out.append(diag_now)
    return jnp.stack(blocks_out), jnp.stack(cross_out), jnp.stack(diag_out)
```

```python
import functools

import jax
import jax.numpy as jnp
from jax import lax
from jax.experimental import pallas as pl
from jax.experimental.pallas import tpu as pltpu
from jax.sharding import PartitionSpec as P

AXES = ("prow", "pcol")
LEVELS = 32766.0
FINE = 64.0
PAD = 16
HIGH = lax.Precision.HIGHEST
VMEM = pl.BlockSpec(memory_space=pltpu.VMEM)
SMEM = pl.BlockSpec(memory_space=pltpu.SMEM)


def params():
    return pltpu.CompilerParams(vmem_limit_bytes=32 * 1024 * 1024)


def cost(flops, moved):
    return pl.CostEstimate(flops=flops, bytes_accessed=moved, transcendentals=0)


def bits_of(size):
    assert size & (size - 1) == 0
    return size.bit_length() - 1


def swap(value, n_row, n_col, row_mask, col_mask):
    pairs = [
        (r * n_col + c, (r ^ row_mask) * n_col + (c ^ col_mask))
        for r in range(n_row)
        for c in range(n_col)
    ]
    return lax.ppermute(value, AXES, pairs)


def encode(block, out_ref):
    rows = block.shape[0]
    top = jnp.maximum(jnp.max(jnp.abs(block), axis=0, keepdims=True), 1e-30)
    step = jnp.ceil(jnp.log2(top) * FINE)
    gain = LEVELS / jnp.exp2(step * (1.0 / FINE))
    out_ref[0:rows, :] = jnp.round(block * gain).astype(jnp.int32).astype(jnp.int16)
    out_ref[rows : rows + PAD, :] = jnp.broadcast_to(step, (PAD, block.shape[1])).astype(jnp.int32).astype(jnp.int16)


def decode(ref):
    rows = ref.shape[0] - PAD
    step = ref[rows : rows + PAD, :].astype(jnp.int32).astype(jnp.float32)[0:1, :]
    gain = jnp.exp2(step * (1.0 / FINE)) * (1.0 / LEVELS)
    return ref[0:rows, :].astype(jnp.int32).astype(jnp.float32) * gain


def live_scale(structure_ref, section, first_row, rows, width):
    group = min(rows, width)
    while rows % group or width % group:
        group //= 2
    parts = []
    for start in range(0, rows, group):
        alive = structure_ref[section, (first_row + start) // width]
        parts.append(jnp.full((group, 1), alive, jnp.int32))
    return jnp.concatenate(parts, axis=0).astype(jnp.float32)


def mask_kernel(flat_ref, structure_ref, panels_ref, out_ref):
    sections, rows, width = panels_ref.shape
    for k in range(sections):
        keep = live_scale(structure_ref, k, flat_ref[0] * rows, rows, width)
        out_ref[:, k * width : (k + 1) * width] = (panels_ref[k].astype(jnp.float32) * keep).astype(jnp.bfloat16)


def strip(where_ref, a_ref, piece_refs, whole_ref):
    rows = piece_refs[0].shape[0]
    for k, piece in enumerate(piece_refs):
        at = pl.multiple_of((where_ref[1] ^ k) * rows, rows)
        whole_ref[pl.ds(at, rows), :] = piece[...]
    return jnp.dot(a_ref[...], whole_ref[...], preferred_element_type=jnp.float32)


def send_kernel(n_piece, where_ref, a_ref, *refs):
    encode(strip(where_ref, a_ref, refs[:n_piece], refs[-1]), refs[n_piece])


def pass_kernel(n_piece, where_ref, a_ref, *refs):
    total = strip(where_ref, a_ref, refs[:n_piece], refs[-1]) + decode(refs[n_piece])
    encode(total, refs[n_piece + 1])


def keep_kernel(n_piece, where_ref, a_ref, *refs):
    refs[n_piece + 1][...] = strip(where_ref, a_ref, refs[:n_piece], refs[-1]) + decode(refs[n_piece])


def chunk_call(body, chunk, row, ainv, pieces, extra, rows, out_shape):
    span = ainv.shape[1]
    wide = pieces[0].shape[1]
    full = lambda shape: pl.BlockSpec(shape, lambda i, s: (0,) * len(shape))
    return pl.pallas_call(
        functools.partial(body, len(pieces)),
        grid_spec=pltpu.PrefetchScalarGridSpec(
            num_scalar_prefetch=1,
            grid=(1,),
            in_specs=[pl.BlockSpec((rows, span), lambda i, s: (s[0], 0))]
            + [full(p.shape) for p in pieces]
            + [full(e.shape) for e in extra],
            out_specs=full(out_shape.shape),
            scratch_shapes=[pltpu.VMEM((span, wide), jnp.bfloat16)],
        ),
        out_shape=out_shape,
        compiler_params=params(),
        cost_estimate=cost(2 * rows * span * wide, 2 * rows * span + 4 * rows * wide + 2 * span * wide),
    )(jnp.stack([chunk, row]), ainv, *pieces, *extra)


def transposed_dot(left, right):
    return lax.dot_general(left, right, (((0,), (0,)), ((), ())), precision=HIGH, preferred_element_type=jnp.float32)


def finish_kernel(n_in, flat_ref, structure_ref, own_ref, factor_ref, couple_ref, *refs):
    arrived, (panels_ref, sums_ref) = refs[:n_in], refs[n_in:]
    sections, rows, width = panels_ref.shape
    total = own_ref[...]
    for ref in arrived:
        total = total + decode(ref)
    blocks, at = [], 0
    for k in range(sections):
        product = total[:, k * width : (k + 1) * width]
        factor = factor_ref[:, k * width : (k + 1) * width].astype(jnp.float32)
        if k:
            product = product + jnp.dot(blocks[-1], couple_ref[k - 1].astype(jnp.float32), precision=HIGH, preferred_element_type=jnp.float32)
        block = -product * live_scale(structure_ref, k, flat_ref[0] * rows, rows, width)
        panels_ref[k] = block
        sums_ref[at : at + width, :] = transposed_dot(factor, block)
        at += width
        if k:
            sums_ref[at : at + width, :] = transposed_dot(blocks[-1], factor)
            at += width
        blocks.append(block)


def tail_kernel(n_core, n_piece, where_ref, dinv_ref, couple_ref, *refs):
    parts, (parent_ref, diag_ref, sums_ref) = refs[:n_core], refs[n_core:]
    rows = parts[0].shape[0] // n_piece
    for h, part in enumerate(parts):
        for k in range(n_piece):
            at = (where_ref[0] ^ h) * (rows * n_piece) + (where_ref[1] ^ k) * rows
            sums_ref[pl.ds(pl.multiple_of(at, 8), rows), :] = part[k * rows : (k + 1) * rows, :]
    sections, width = dinv_ref.shape[0], dinv_ref.shape[1]
    diag = dinv_ref[0] - sums_ref[0:width, :]
    diag_ref[0] = diag
    for k in range(1, sections):
        own = sums_ref[(2 * k - 1) * width : 2 * k * width, :]
        shared = sums_ref[2 * k * width : (2 * k + 1) * width, :]
        link = couple_ref[k - 1].astype(jnp.float32)
        cross = -(shared + jnp.dot(diag, link, precision=HIGH, preferred_element_type=jnp.float32))
        diag = dinv_ref[k] - own - transposed_dot(link, cross)
        parent_ref[k - 1] = cross
        diag_ref[k] = diag


def shards(n_row, n_col, ainv, panels, structure, dinv, couple):
    row = lax.axis_index("prow")
    col = lax.axis_index("pcol")
    flat = jnp.reshape(row * n_col + col, (1,))
    sections, seg, width = panels.shape
    wide = sections * width
    height = ainv.shape[0]
    rows = height // n_col
    f32 = jnp.float32

    factor = pl.pallas_call(
        mask_kernel,
        in_specs=[SMEM, SMEM, VMEM],
        out_specs=VMEM,
        out_shape=jax.ShapeDtypeStruct((seg, wide), jnp.bfloat16),
        compiler_params=params(),
        cost_estimate=cost(seg * wide, 4 * seg * wide),
    )(flat, structure, panels)

    moved = lax.ppermute(factor, AXES, [(s, (s % n_row) * n_col + s // n_row) for s in range(n_row * n_col)])
    pieces = {0: moved}
    for bit in reversed(range(bits_of(n_row))):
        mask = 1 << bit
        held = sorted(pieces)
        if len(held) == 1:
            got = [swap(pieces[held[0]], n_row, n_col, mask, 0)]
        else:
            got = [swap(pieces[h], n_row, n_col, mask, 0) for h in held]
        for h, value in zip(held, got):
            pieces[h ^ mask] = value
    pieces = [pieces[k] for k in range(n_row)]

    coded = jax.ShapeDtypeStruct((rows + PAD, wide), jnp.int16)
    plain = jax.ShapeDtypeStruct((rows, wide), f32)
    far = [2 * k for k in reversed(range(n_col // 2))]
    near = {}
    for k in far:
        out = chunk_call(send_kernel, col ^ (k + 1), row, ainv, pieces, (), rows, coded)
        near[k] = swap(out, n_row, n_col, 0, 1)
    arrived = []
    for k in far[:-1]:
        out = chunk_call(pass_kernel, col ^ k, row, ainv, pieces, (near[k],), rows, coded)
        arrived.append(swap(out, n_row, n_col, 0, k))
    own = chunk_call(keep_kernel, col, row, ainv, pieces, (near[0],), rows, plain)

    n_sum = (2 * sections - 1) * width
    blocks, sums = pl.pallas_call(
        functools.partial(finish_kernel, len(arrived)),
        in_specs=[SMEM, SMEM] + [VMEM] * (3 + len(arrived)),
        out_specs=[VMEM, VMEM],
        out_shape=[jax.ShapeDtypeStruct((sections, rows, width), f32), jax.ShapeDtypeStruct((n_sum, width), f32)],
        compiler_params=params(),
        cost_estimate=cost(2 * 7 * rows * width * width * 6, 8 * rows * wide),
    )(flat, structure, own, factor, couple, *arrived)

    def part(value, index, count):
        size = value.shape[0] // count
        return lax.dynamic_slice_in_dim(value, index * size, size, 0)

    core = row & 1
    half = part(sums, core, 2) + swap(part(sums, core ^ 1, 2), n_row, n_col, 1, 0)
    quad = [(0, 0), (0, 1), (2, 0), (2, 1)]
    spot = (row & 2) | (col & 1)
    got = [part(half, spot, 4)] + [swap(part(half, spot ^ k, 4), n_row, n_col, *quad[k]) for k in (1, 2, 3)]
    total = (got[0] + got[1]) + (got[2] + got[3])
    rest = [(0, 1 << b) for b in range(1, bits_of(n_col))] + [(1 << b, 0) for b in range(2, bits_of(n_row))]
    while rest:
        masks, rest = rest[:2], rest[2:]
        got = [total, swap(total, n_row, n_col, *masks[0])]
        if len(masks) == 2:
            both = (masks[0][0] | masks[1][0], masks[0][1] | masks[1][1])
            got += [swap(total, n_row, n_col, *masks[1]), swap(total, n_row, n_col, *both)]
            total = (got[0] + got[1]) + (got[2] + got[3])
        else:
            total = got[0] + got[1]
    half = jnp.concatenate([total] + [swap(total, n_row, n_col, *quad[k]) for k in (1, 2, 3)], axis=0)
    other = swap(half, n_row, n_col, 1, 0)

    parent, diag = pl.pallas_call(
        functools.partial(tail_kernel, 2, 4),
        in_specs=[SMEM] + [VMEM] * 4,
        out_specs=[VMEM, VMEM],
        out_shape=[jax.ShapeDtypeStruct((sections - 1, width, width), f32), jax.ShapeDtypeStruct((sections, width, width), f32)],
        scratch_shapes=[pltpu.VMEM((n_sum, width), f32)],
        compiler_params=params(),
        cost_estimate=cost(2 * 4 * width**3 * 6, 8 * n_sum * width),
    )(jnp.stack([core, spot]), dinv, couple, half, other)
    return blocks, parent, diag


def solution(mesh):
    body = functools.partial(shards, mesh.shape["prow"], mesh.shape["pcol"])
    return jax.shard_map(
        body,
        mesh=mesh,
        in_specs=(P("prow", "pcol"), P(None, AXES, None), P(), P(), P()),
        out_specs=(P(None, AXES, None), P(), P()),
        check_vma=False,
    )
```
